32 devices in a mesh: groups: 2 (over x), tensor: 16 (over z, y, core).
Axes of the slice: x: 2, y: 2, z: 4, core: 2. Of those that a mesh axis runs over, the one named last changes fastest.
Arguments:
- tokens: bfloat16 [64, 8192], P(('groups', 'tensor')), parts along dimension 0, may hold values from -6 to 6
- cotangent: bfloat16 [64, 8192], P(('groups', 'tensor')), parts along dimension 0, may hold values from -6 to 6
- up_blocks: bfloat16 [512, 128, 128], P('tensor'), may hold values from -0.1875 to 0.1875
- gate_blocks: bfloat16 [512, 128, 128], P('tensor'), may hold values from -0.1875 to 0.1875
- down_blocks: bfloat16 [512, 128, 128], P('tensor'), may hold values from -0.21875 to 0.21875
- up_layout: int32 [512], P('tensor'), may hold values from 0 to 191, as said below
- gate_layout: int32 [512], P('tensor'), may hold values from 0 to 191, as said below
- down_layout: int32 [512], P('tensor'), may hold values from 0 to 191, as said below
- live_counts: int32 [3, 16], P(None, 'tensor'), may hold values from 4 to 32, as said below
Outputs:
- output: bfloat16 [64, 8192], P(('groups', 'tensor')), parts along dimension 0
- grad_tokens: bfloat16 [64, 8192], P(('groups', 'tensor')), parts along dimension 0
- grad_up: bfloat16 [1024, 128, 128], P(('groups', 'tensor')), parts along dimension 0
- grad_gate: bfloat16 [1024, 128, 128], P(('groups', 'tensor')), parts along dimension 0
- grad_down: bfloat16 [1024, 128, 128], P(('groups', 'tensor')), parts along dimension 0
The draws below stay inside these ranges and needn't reach their ends.
There are 2 independent parts, one for each index of `groups`. The reference program is written for one: setup_inputs(seed, part) draws one part's arguments, and reference() takes and returns one part's arrays. A program takes and returns all parts, laid end to end along the dimension named above; an argument that names none is the same for every part. Nothing has to cross between parts.
Inputs may be any that keep to these rules, and one draw needn't show every extreme that they name: `up_layout`: within the 32 slots of one owner the codes of one matrix are all different. `gate_layout`: within the 32 slots of one owner the codes of one matrix are all different. `down_layout`: within the 32 slots of one owner the codes of one matrix are all different. `live_counts`: in each of the three rows some owner has exactly 32 live slots; slots past an owner's count hold blocks that are not used.
All inputs are finite; a program needn't handle non-finite values.
Results may differ from the reference program's by a relative error of at most 0.0051.
Values may be sent and summed in bfloat16 or wider, within the bound.
A program may use at most 64 MiB of HBM per device.

```python
import jax
import jax.numpy as jnp
from jax import lax

D = 8192
BLOCK = 128
HB_DEV = 3
NB_DEV = 32
TOKENS = 32
FF = 6144
DB = 64
N_TENSOR = 16


def layout_codes(key, salt):
    owner_keys = jax.random.split(jax.random.fold_in(key, salt), N_TENSOR)

    def one_owner(owner_key):
        return jax.random.permutation(owner_key, DB * HB_DEV)[:NB_DEV]
    return jax.vmap(one_owner)(owner_keys).reshape(-1).astype(jnp.int32)


def draw_up_layout(key, part):
    return layout_codes(key, 11)


def draw_gate_layout(key, part):
    return layout_codes(key, 12)


def draw_down_layout(key, part):
    return layout_codes(key, 13)


def draw_live_counts(key, part):
    lowest = max(1, NB_DEV // 8)
    first_key, second_key = jax.random.split(jax.random.fold_in(key, 17))
    counts = jax.random.randint(first_key, (3, N_TENSOR), lowest, NB_DEV + 1)
    busiest = jax.random.randint(second_key, (3, 1), 0, N_TENSOR)
    owners = jnp.arange(N_TENSOR)[None, :]
    return jnp.where(owners == busiest, NB_DEV, counts).astype(jnp.int32)


def level_of(rng, dims, pieces, low, high):
    factor_of = 1.0
    for dim, shards_of in pieces:
        heights = jax.random.uniform(jax.random.fold_in(jax.random.fold_in(rng, 6), dim), (shards_of,), jnp.float32, low / len(pieces), high / len(pieces))
        factor_of = factor_of * jnp.repeat(jnp.exp(heights), dims[dim] // shards_of).reshape((-1,) + (1,) * (len(dims) - 1 - dim))
    return factor_of


def bell_draw(rng, extent, deviation, most, pieces=(), dtype=jnp.bfloat16):
    values = jax.random.normal(rng, extent, jnp.float32) * deviation
    if len(pieces) > 0:
        values = level_of(rng, extent, pieces, -0.22, 0.18) * values
    return jnp.clip(values, min=-most, max=most).astype(dtype)


def setup_inputs(seed: int = 0, part: int = 0) -> dict:
    seeds = jax.random.split(jax.random.key(seed), 10)
    part_splits = jax.random.split(jax.random.fold_in(seeds[9], part), 10)
    return {
        "tokens": bell_draw(part_splits[0], (TOKENS, D), 1.0, 6.0, ((0, 16),)),
        "cotangent": bell_draw(part_splits[1], (TOKENS, D), 1.0, 6.0, ((0, 16),)),
        "up_blocks": bell_draw(seeds[2], (N_TENSOR * NB_DEV, BLOCK, BLOCK), (D // 8) ** -0.5, 0.1875, ((0, 16),)),
        "gate_blocks": bell_draw(seeds[3], (N_TENSOR * NB_DEV, BLOCK, BLOCK), (D // 8) ** -0.5, 0.1875, ((0, 16),)),
        "down_blocks": bell_draw(seeds[4], (N_TENSOR * NB_DEV, BLOCK, BLOCK), (FF // 8) ** -0.5, 0.21875, ((0, 16),)),
        "up_layout": draw_up_layout(jax.random.fold_in(seeds[9], 71), part),
        "gate_layout": draw_gate_layout(jax.random.fold_in(seeds[9], 71), part),
        "down_layout": draw_down_layout(jax.random.fold_in(seeds[9], 71), part),
        "live_counts": draw_live_counts(jax.random.fold_in(seeds[9], 71), part),
    }


def slot_tables(layout, count, major_size):
    slot_total = layout.shape[0]
    major = (layout // HB_DEV).astype(jnp.int32)
    minor = (layout % HB_DEV).astype(jnp.int32)
    live_mask = (jnp.arange(slot_total) < count).astype(jnp.float32)
    major_hot = (major[:, None] == jnp.arange(major_size)[None, :]).astype(jnp.float32)
    minor_hot = (minor[:, None] == jnp.arange(HB_DEV)[None, :]).astype(jnp.float32)
    return major, minor, live_mask, major_hot, minor_hot


def owner_pass(x_full, dy_full, up_blk, gate_blk, down_blk, up_lay, gate_lay, down_lay, count_trio):
    highest = lax.Precision.HIGHEST
    f32 = jnp.float32
    row_total = x_full.shape[0]
    block_size = up_blk.shape[1]
    width_blocks = x_full.shape[1] // block_size
    x_split = x_full.reshape(row_total, width_blocks, block_size)
    dy_split = dy_full.reshape(row_total, width_blocks, block_size)
    up_major, up_minor, up_live, up_rowhot, up_hidhot = slot_tables(up_lay, count_trio[0], width_blocks)
    gate_major, gate_minor, gate_live, gate_rowhot, gate_hidhot = slot_tables(gate_lay, count_trio[1], width_blocks)
    down_major, down_minor, down_live, down_colhot, down_hidhot = slot_tables(down_lay, count_trio[2], width_blocks)
    w_up = up_blk * up_live[:, None, None].astype(jnp.bfloat16)
    w_gate = gate_blk * gate_live[:, None, None].astype(jnp.bfloat16)
    w_down = down_blk * down_live[:, None, None].astype(jnp.bfloat16)
    x_up = jnp.take(x_split, up_major, axis=1).astype(f32)
    x_gate = jnp.take(x_split, gate_major, axis=1).astype(f32)
    up_terms = jnp.einsum('tsi,sij->tsj', x_up, w_up.astype(f32), precision=highest)
    gate_terms = jnp.einsum('tsi,sij->tsj', x_gate, w_gate.astype(f32), precision=highest)
    up_value = jnp.einsum('tsj,sh->thj', up_terms, up_hidhot, precision=highest)
    gate_value = jnp.einsum('tsj,sh->thj', gate_terms, gate_hidhot, precision=highest)
    sig = 1.0 / (1.0 + jnp.exp(-gate_value))
    act = gate_value * sig
    hidden = (act * up_value).astype(jnp.bfloat16)
    hid_down = jnp.take(hidden, down_minor, axis=1).astype(f32)
    out_terms = jnp.einsum('tsj,sjk->tsk', hid_down, w_down.astype(f32), precision=highest)
    partial_out = jnp.einsum('tsk,sc->tck', out_terms, down_colhot, precision=highest).reshape(row_total, -1)
    dy_down = jnp.take(dy_split, down_major, axis=1).astype(f32)
    dh_terms = jnp.einsum('tsk,sjk->tsj', dy_down, w_down.astype(f32), precision=highest)
    d_hidden = jnp.einsum('tsj,sh->thj', dh_terms, down_hidhot, precision=highest)
    d_up = (d_hidden * act).astype(jnp.bfloat16)
    d_gate = (d_hidden * up_value * sig * (1.0 + gate_value * (1.0 - sig))).astype(jnp.bfloat16)
    dup_slots = jnp.take(d_up, up_minor, axis=1).astype(f32)
    dgate_slots = jnp.take(d_gate, gate_minor, axis=1).astype(f32)
    dx_up = jnp.einsum('tsj,sij->tsi', dup_slots, w_up.astype(f32), precision=highest)
    dx_gate = jnp.einsum('tsj,sij->tsi', dgate_slots, w_gate.astype(f32), precision=highest)
    partial_dx = jnp.einsum('tsi,sr->tri', dx_up, up_rowhot, precision=highest)
    partial_dx = partial_dx + jnp.einsum('tsi,sr->tri', dx_gate, gate_rowhot, precision=highest)
    partial_dx = partial_dx.reshape(row_total, -1)
    grad_up = (jnp.einsum('tsi,tsj->sij', x_up, dup_slots, precision=highest) * up_live[:, None, None]).astype(jnp.bfloat16)
    grad_gate = (jnp.einsum('tsi,tsj->sij', x_gate, dgate_slots, precision=highest) * gate_live[:, None, None]).astype(jnp.bfloat16)
    grad_down = (jnp.einsum('tsj,tsk->sjk', hid_down, dy_down, precision=highest) * down_live[:, None, None]).astype(jnp.bfloat16)
    return partial_out, partial_dx, grad_up, grad_gate, grad_down


def reference(tokens, cotangent, up_blocks, gate_blocks, down_blocks, up_layout, gate_layout, down_layout, live_counts):
    block_size = up_blocks.shape[1]
    owners = live_counts.shape[1]
    slot_count = up_blocks.shape[0] // owners

    def split_owner(array):
        return array.reshape((owners, slot_count) + array.shape[1:])

    per_owner = (split_owner(up_blocks), split_owner(gate_blocks), split_owner(down_blocks),
                 split_owner(up_layout), split_owner(gate_layout), split_owner(down_layout),
                 jnp.transpose(live_counts))

    def one_owner(carry, items):
        partial_out, partial_dx, grad_up, grad_gate, grad_down = owner_pass(tokens, cotangent, *items)
        return (carry[0] + partial_out, carry[1] + partial_dx), (grad_up, grad_gate, grad_down)

    start = (jnp.zeros(tokens.shape, jnp.float32), jnp.zeros(tokens.shape, jnp.float32))
    totals, grads = lax.scan(one_owner, start, per_owner)
    flat_shape = (owners * slot_count, block_size, block_size)
    return (totals[0].astype(jnp.bfloat16), totals[1].astype(jnp.bfloat16),
            grads[0].reshape(flat_shape), grads[1].reshape(flat_shape), grads[2].reshape(flat_shape))
```

```python
import functools

import jax
import jax.numpy as jnp
from jax import lax
from jax.experimental import pallas as pl
from jax.experimental.pallas import tpu as pltpu
from jax.sharding import PartitionSpec as P

HB = 3
BF16 = jnp.bfloat16
F32 = jnp.float32
NT = (((1,), (1,)), ((), ()))
TN = (((0,), (0,)), ((), ()))


def third(code):
    return (code * 171) >> 9


def layer_kernel(
    n, lay_ref, cnt_ref, tok_ref, cot_ref, wu_hbm, wg_hbm, wd_hbm,
    xg, yg, hid, dup, dgt, outp, dxp,
    wu, wg, wd, mx, terms, terms2, inv_v, inv_s, po, own, r1, t2, r2, t3, r3,
    wsem, isem, gsend, grecv, s1, q1, lsem, s2, q2, s3, q3,
):
    nz = n // 4
    db = xg.shape[0]
    rows = xg.shape[2]
    bs = xg.shape[3]
    tt = n * rows
    slots = wu.shape[0]
    me = lax.axis_index("tensor")
    z, y, p = me // 4, (me // 2) % 2, me % 2
    sib = me + 1 - 2 * p
    pair = me + 2 - 4 * y
    zs = [(z + k) % nz for k in range(nz)]

    def at(zz, yy, pp):
        return zz * 4 + yy * 2 + pp

    def dev(j):
        return {"tensor": j}

    wcopies = [
        pltpu.make_async_copy(src, dst, wsem.at[i])
        for i, (src, dst) in enumerate(((wu_hbm, wu), (wg_hbm, wg), (wd_hbm, wd)))
    ]
    for c in wcopies:
        c.start()

    barrier = pltpu.get_barrier_semaphore()
    for j in [at(zz, y, p) for zz in zs[1:]] + [pair, sib]:
        pl.semaphore_signal(
            barrier, inc=1, device_id=dev(j), device_id_type=pl.DeviceIdType.MESH
        )

    for c in range(db):
        xg[c, me] = tok_ref[:, c * bs:(c + 1) * bs]
        yg[c, me] = cot_ref[:, c * bs:(c + 1) * bs]

    pl.semaphore_wait(barrier, nz - 1 + 2)

    gbuf = (xg, yg)
    nsend = [0, 0]
    pending = []

    def gsendto(a, chunk, j):
        c = pltpu.make_async_remote_copy(
            src_ref=gbuf[a].at[:, chunk],
            dst_ref=gbuf[a].at[:, chunk],
            send_sem=gsend.at[a, nsend[a]],
            recv_sem=grecv.at[a, chunk],
            device_id=dev(j),
            device_id_type=pl.DeviceIdType.MESH,
        )
        nsend[a] += 1
        c.start()
        pending.append(c)

    def gwait(a, chunk):
        pltpu.make_async_remote_copy(
            src_ref=gbuf[a].at[:, chunk],
            dst_ref=gbuf[a].at[:, chunk],
            send_sem=gsend.at[a, 0],
            recv_sem=grecv.at[a, chunk],
            device_id=dev(sib),
            device_id_type=pl.DeviceIdType.MESH,
        ).wait_recv()

    for a in range(2):
        for zz in zs[1:]:
            gsendto(a, me, at(zz, y, p))
        gsendto(a, me, pair)
        gsendto(a, me, sib)

    lane = lax.broadcasted_iota(jnp.int32, (8, 256), 1)
    for m in range(3):
        tab = jnp.full((8, 256), slots, jnp.int32)
        for s in range(slots):
            code = jnp.where(s < cnt_ref[m, 0], lay_ref[m, s], -1)
            tab = jnp.where(lane == code, s, tab)
        inv_v[m] = tab
    icopy = pltpu.make_async_copy(inv_v, inv_s, isem.at[0])
    icopy.start()
    terms[slots] = jnp.zeros((tt, bs), F32)
    terms2[slots] = jnp.zeros((tt, bs), F32)

    def forward_z(a):
        for zz in zs[1:]:
            gwait(a, at(zz, y, p))
            gsendto(a, at(zz, y, p), pair)
            gsendto(a, at(zz, y, p), sib)

    def forward_y(a):
        for zz in zs:
            gwait(a, at(zz, 1 - y, p))
            gsendto(a, at(zz, 1 - y, p), sib)

    def finish(a):
        for zz in zs:
            gwait(a, at(zz, y, 1 - p))
            gwait(a, at(zz, 1 - y, 1 - p))

    def contract(src, m, weights, transposed):
        view = src.reshape(db, tt, bs)

        def pick(s, carry):
            code = lay_ref[m, s]
            major = third(code)
            minor = jnp.where(s < cnt_ref[m, 0], code - 3 * major, HB)
            rows_s = view[major]
            for h in range(HB):
                mx[s, h * tt:(h + 1) * tt, :] = jnp.where(
                    minor == h, rows_s, jnp.zeros_like(rows_s)
                )
            return carry

        lax.fori_loop(0, slots, pick, 0, unroll=True)
        acc = jnp.zeros((HB * tt, bs), F32)
        for s in range(slots):
            if transposed:
                acc += lax.dot_general(mx[s], weights[s], NT, preferred_element_type=F32)
            else:
                acc += jnp.dot(mx[s], weights[s], preferred_element_type=F32)
        return acc

    def scatter(a, tables):
        pov = po.at[a].reshape(db, tt, bs)

        def place(c, carry):
            total = jnp.zeros((tt, bs), F32)
            for m, source in tables:
                for h in range(HB):
                    total += source[inv_s[m, 0, c * HB + h]]
            pov[c] = total.astype(BF16)
            return carry

        lax.fori_loop(0, db, place, 0, unroll=4)

    flat = (db * rows, bs)
    order = zs[1:] + zs[:1]

    def remote(src, dst, send, recv, j):
        return pltpu.make_async_remote_copy(
            src_ref=src, dst_ref=dst, send_sem=send, recv_sem=recv,
            device_id=dev(j), device_id_type=pl.DeviceIdType.MESH,
        )

    def copy1(a, zz, yy):
        return remote(
            po.at[a, :, at(zz, yy, 1 - p)], r1.at[a, zz, yy],
            s1.at[a, zz, yy], q1.at[a, zz, yy], sib,
        )

    def local(a, zz, yy):
        return pltpu.make_async_copy(
            po.at[a, :, at(zz, yy, p)], own.at[a, zz, yy], lsem.at[a, zz, yy]
        )

    def copy2(a, zz):
        return remote(t2.at[a, zz], r2.at[a, zz], s2.at[a, zz], q2.at[a, zz], pair)

    def copy3(a, zz, slot):
        return remote(
            t3.at[a, zz], r3.at[a, slot], s3.at[a, zz], q3.at[a, slot], at(zz, y, p)
        )

    def reduce_core(a):
        for yy in (1 - y, y):
            for zz in order:
                copy1(a, zz, yy).start()
                local(a, zz, yy).start()

    def load(ref, *idx):
        return ref.at[idx].reshape(*flat)[...].astype(F32)

    def store(ref, value, *idx):
        ref.at[idx].reshape(*flat)[...] = value.astype(BF16)

    def reduce_pair(a):
        for zz in order:
            copy1(a, zz, 1 - y).wait_recv()
            local(a, zz, 1 - y).wait()
            store(t2, load(own, a, zz, 1 - y) + load(r1, a, zz, 1 - y), a, zz)
            copy2(a, zz).start()

    def reduce_z(a):
        for zz in order:
            copy1(a, zz, y).wait_recv()
            local(a, zz, y).wait()
            copy2(a, zz).wait_recv()
            total = load(own, a, zz, y) + load(r1, a, zz, y) + load(r2, a, zz)
            if zz is zs[0]:
                return total
            store(t3, total, a, zz)
            copy3(a, zz, z).start()

    def reduce_end(a, total, result):
        for zz in zs[1:]:
            copy3(a, zz, zz).wait_recv()
            total += load(r3, a, zz)
        result.reshape(*flat)[...] = total.astype(BF16)
        for zz in order:
            for yy in (0, 1):
                copy1(a, zz, yy).wait_send()
            copy2(a, zz).wait_send()
        for zz in zs[1:]:
            copy3(a, zz, z).wait_send()

    def expand(weights, src, m, dst, dims):
        for s in range(slots):
            minor = lay_ref[m, s] - 3 * third(lay_ref[m, s])
            dst[s] = lax.dot_general(
                src[minor], weights[s], dims, preferred_element_type=F32
            )

    forward_z(0)
    forward_y(0)
    forward_z(1)
    finish(0)
    wcopies[0].wait()
    up = contract(xg, 0, wu, False)
    wcopies[1].wait()
    gate = contract(xg, 1, wg, False)
    sig = 1.0 / (1.0 + jnp.exp(-gate))
    act = gate * sig
    hid.reshape(HB * tt, bs)[...] = (act * up).astype(BF16)
    forward_y(1)
    wcopies[2].wait()
    icopy.wait()
    expand(wd, hid, 2, terms, (((1,), (0,)), ((), ())))
    scatter(0, ((2, terms),))
    reduce_core(0)
    finish(1)
    d_hidden = contract(yg, 2, wd, True)
    dup.reshape(HB * tt, bs)[...] = (d_hidden * act).astype(BF16)
    dgt.reshape(HB * tt, bs)[...] = (
        d_hidden * up * sig * (1.0 + gate * (1.0 - sig))
    ).astype(BF16)
    reduce_pair(0)
    expand(wu, dup, 0, terms, NT)
    expand(wg, dgt, 1, terms2, NT)
    scatter(1, ((0, terms), (1, terms2)))
    reduce_core(1)
    total0 = reduce_z(0)
    reduce_pair(1)
    total1 = reduce_z(1)
    reduce_end(0, total0, outp)
    reduce_end(1, total1, dxp)
    for c in pending:
        c.wait_send()


def grads_kernel(
    per, lay_ref, cnt_ref, xg, yg, hid, dup, dgt, outp, dxp,
    out, dx, gu, gg, gd,
):
    step = pl.program_id(0)
    db, _, bs = outp.shape

    @pl.when(step == 0)
    def _():
        for c in range(db):
            out[:, c * bs:(c + 1) * bs] = outp[c]
            dx[:, c * bs:(c + 1) * bs] = dxp[c]

    for i in range(per):
        s = step * per + i
        for m, grad in ((0, gu), (1, gg), (2, gd)):
            code = lay_ref[m, s]
            major = third(code)
            minor = code - 3 * major
            if m == 2:
                lhs, rhs = hid[minor], yg[major]
            else:
                lhs, rhs = xg[major], (dup, dgt)[m][minor]
            lhs = jnp.where(s < cnt_ref[m, 0], lhs, jnp.zeros_like(lhs))
            grad[i] = lax.dot_general(
                lhs, rhs, TN, preferred_element_type=F32
            ).astype(BF16)


def local_part(n, tokens, cotangent, wu, wg, wd, lu, lg, ld, counts):
    rows, width = tokens.shape
    slots, bs, _ = wu.shape
    db, tt, nz = width // bs, n * rows, n // 4
    layout = jnp.stack([lu, lg, ld])
    vm = pl.BlockSpec(memory_space=pltpu.VMEM)
    sm = pl.BlockSpec(memory_space=pltpu.SMEM)
    hbm = pl.BlockSpec(memory_space=pl.ANY)
    shape = jax.ShapeDtypeStruct
    dma = pltpu.SemaphoreType.DMA
    part = (nz, db, rows, bs)
    xg, yg, hid, dup, dgt, outp, dxp = pl.pallas_call(
        functools.partial(layer_kernel, n),
        out_shape=[shape((db, n, rows, bs), BF16)] * 2
        + [shape((HB, tt, bs), BF16)] * 3
        + [shape((db, rows, bs), BF16)] * 2,
        in_specs=[sm, sm, vm, vm, hbm, hbm, hbm],
        out_specs=[vm] * 7,
        scratch_shapes=[
            pltpu.VMEM((slots, bs, bs), BF16),
            pltpu.VMEM((slots, bs, bs), BF16),
            pltpu.VMEM((slots, bs, bs), BF16),
            pltpu.VMEM((slots, HB * tt, bs), BF16),
            pltpu.VMEM((slots + 1, tt, bs), F32),
            pltpu.VMEM((slots + 1, tt, bs), F32),
            pltpu.VMEM((3, 8, 256), jnp.int32),
            pltpu.SMEM((3, 8, 256), jnp.int32),
            pltpu.VMEM((2, db, n, rows, bs), BF16),
            pltpu.VMEM((2, nz, 2, db, rows, bs), BF16),
            pltpu.VMEM((2, nz, 2, db, rows, bs), BF16),
            pltpu.VMEM((2,) + part, BF16),
            pltpu.VMEM((2,) + part, BF16),
            pltpu.VMEM((2,) + part, BF16),
            pltpu.VMEM((2,) + part, BF16),
            dma((3,)), dma((1,)), dma((2, n)), dma((2, n)),
            dma((2, nz, 2)), dma((2, nz, 2)), dma((2, nz, 2)),
            dma((2, nz)), dma((2, nz)), dma((2, nz)), dma((2, nz)),
        ],
        compiler_params=pltpu.CompilerParams(
            collective_id=0, has_side_effects=True, vmem_limit_bytes=48 << 20
        ),
        name="layer",
    )(layout, counts, tokens, cotangent, wu, wg, wd)
    xg = xg.reshape(db, tt, bs)
    yg = yg.reshape(db, tt, bs)
    per = slots // 4
    block = pl.BlockSpec((per, bs, bs), lambda i: (i, 0, 0))
    row = pl.BlockSpec((rows, width), lambda i: (0, 0))

    def whole(a):
        return pl.BlockSpec(a.shape, lambda i: (0,) * a.ndim)

    rest = (xg, yg, hid, dup, dgt, outp, dxp)
    return pl.pallas_call(
        functools.partial(grads_kernel, per),
        grid=(4,),
        out_shape=[shape((rows, width), BF16)] * 2 + [shape((slots, bs, bs), BF16)] * 3,
        in_specs=[sm, sm] + [whole(a) for a in rest],
        out_specs=[row, row, block, block, block],
        compiler_params=pltpu.CompilerParams(vmem_limit_bytes=48 << 20),
        name="grads",
    )(layout, counts, *rest)


def solution(mesh):
    n = mesh.shape["tensor"]
    both = ("groups", "tensor")
    return jax.shard_map(
        functools.partial(local_part, n),
        mesh=mesh,
        in_specs=(
            P(both, None), P(both, None),
            P("tensor", None, None), P("tensor", None, None), P("tensor", None, None),
            P("tensor"), P("tensor"), P("tensor"), P(None, "tensor"),
        ),
        out_specs=(
            P(both, None), P(both, None),
            P(both, None, None), P(both, None, None), P(both, None, None),
        ),
        check_vma=False,
    )
```

```python
import functools

import jax
import jax.numpy as jnp
from jax import lax
from jax.experimental import pallas as pl
from jax.experimental.pallas import tpu as pltpu
from jax.sharding import PartitionSpec as P

HB = 3
BF16 = jnp.bfloat16
F32 = jnp.float32
NT = (((1,), (1,)), ((), ()))
TN = (((0,), (0,)), ((), ()))


def third(code):
    return (code * 171) >> 9


def layer_kernel(
    n, lu_hbm, lg_hbm, ld_hbm, cnt_hbm, tok_hbm, cot_hbm, wu_hbm, wg_hbm, wd_hbm,
    xg_hbm, yg_hbm, hid_hbm, dup_hbm, dgt_hbm, outp, dxp,
    xg, yg, hid, dup, dgt, lay_ref, cnt_ref, tok_ref, cot_ref, wu, wg, wd, mx, terms, terms2, inv_v, inv_s, po, own, r1, t2, r2, t3, r3,
    osem, asem, wsem, isem, gsend, grecv, s1, q1, lsem, s2, q2, s3, q3,
):
    nz = n // 4
    db = xg.shape[0]
    rows = xg.shape[2]
    bs = xg.shape[3]
    tt = n * rows
    slots = wu.shape[0]
    me = lax.axis_index("tensor")
    z, y, p = me // 4, (me // 2) % 2, me % 2
    sib = me + 1 - 2 * p
    pair = me + 2 - 4 * y
    zs = [(z + k) % nz for k in range(nz)]

    def at(zz, yy, pp):
        return zz * 4 + yy * 2 + pp

    def dev(j):
        return {"tensor": j}

    acopies = [
        pltpu.make_async_copy(src, dst, asem.at[i])
        for i, (src, dst) in enumerate((
            (tok_hbm, tok_ref), (cot_hbm, cot_ref), (cnt_hbm, cnt_ref),
            (lu_hbm, lay_ref.at[0]), (lg_hbm, lay_ref.at[1]), (ld_hbm, lay_ref.at[2]),
        ))
    ]
    for c in acopies:
        c.start()
    wcopies = [
        pltpu.make_async_copy(src, dst, wsem.at[i])
        for i, (src, dst) in enumerate(((wu_hbm, wu), (wg_hbm, wg), (wd_hbm, wd)))
    ]
    for c in wcopies:
        c.start()

    barrier = pltpu.get_barrier_semaphore()
    for j in [at(zz, y, p) for zz in zs[1:]] + [pair, sib]:
        pl.semaphore_signal(
            barrier, inc=1, device_id=dev(j), device_id_type=pl.DeviceIdType.MESH
        )

    for c in acopies[:2]:
        c.wait()
    for c in range(db):
        xg[c, me] = tok_ref[:, c * bs:(c + 1) * bs]
        yg[c, me] = cot_ref[:, c * bs:(c + 1) * bs]

    pl.semaphore_wait(barrier, nz - 1 + 2)

    gbuf = (xg, yg)
    nsend = [0, 0]
    pending = []

    def gsendto(a, chunk, j):
        c = pltpu.make_async_remote_copy(
            src_ref=gbuf[a].at[:, chunk],
            dst_ref=gbuf[a].at[:, chunk],
            send_sem=gsend.at[a, nsend[a]],
            recv_sem=grecv.at[a, chunk],
            device_id=dev(j),
            device_id_type=pl.DeviceIdType.MESH,
        )
        nsend[a] += 1
        c.start()
        pending.append(c)

    def gwait(a, chunk):
        pltpu.make_async_remote_copy(
            src_ref=gbuf[a].at[:, chunk],
            dst_ref=gbuf[a].at[:, chunk],
            send_sem=gsend.at[a, 0],
            recv_sem=grecv.at[a, chunk],
            device_id=dev(sib),
            device_id_type=pl.DeviceIdType.MESH,
        ).wait_recv()

    for a in range(2):
        for zz in zs[1:]:
            gsendto(a, me, at(zz, y, p))
        gsendto(a, me, pair)
        gsendto(a, me, sib)

    for c in acopies[2:]:
        c.wait()
    lane = lax.broadcasted_iota(jnp.int32, (8, 256), 1)
    for m in range(3):
        tab = jnp.full((8, 256), slots, jnp.int32)
        for s in range(slots):
            code = jnp.where(s < cnt_ref[m], lay_ref[m, s], -1)
            tab = jnp.where(lane == code, s, tab)
        inv_v[m] = tab
    icopy = pltpu.make_async_copy(inv_v, inv_s, isem.at[0])
    icopy.start()
    terms[slots] = jnp.zeros((tt, bs), F32)
    terms2[slots] = jnp.zeros((tt, bs), F32)

    def forward_z(a):
        for zz in zs[1:]:
            gwait(a, at(zz, y, p))
            gsendto(a, at(zz, y, p), pair)
            gsendto(a, at(zz, y, p), sib)

    def forward_y(a):
        for zz in zs:
            gwait(a, at(zz, 1 - y, p))
            gsendto(a, at(zz, 1 - y, p), sib)

    def finish(a):
        for zz in zs:
            gwait(a, at(zz, y, 1 - p))
            gwait(a, at(zz, 1 - y, 1 - p))

    def contract(src, m, weights, transposed):
        view = src.reshape(db, tt, bs)

        def pick(s, carry):
            code = lay_ref[m, s]
            major = third(code)
            minor = jnp.where(s < cnt_ref[m], code - 3 * major, HB)
            rows_s = view[major]
            for h in range(HB):
                mx[s, h * tt:(h + 1) * tt, :] = jnp.where(
                    minor == h, rows_s, jnp.zeros_like(rows_s)
                )
            return carry

        lax.fori_loop(0, slots, pick, 0, unroll=True)
        acc = jnp.zeros((HB * tt, bs), F32)
        for s in range(slots):
            if transposed:
                acc += lax.dot_general(mx[s], weights[s], NT, preferred_element_type=F32)
            else:
                acc += jnp.dot(mx[s], weights[s], preferred_element_type=F32)
        return acc

    def scatter(a, tables):
        pov = po.at[a].reshape(db, tt, bs)

        def place(c, carry):
            total = jnp.zeros((tt, bs), F32)
            for m, source in tables:
                for h in range(HB):
                    total += source[inv_s[m, 0, c * HB + h]]
            pov[c] = total.astype(BF16)
            return carry

        lax.fori_loop(0, db, place, 0, unroll=4)

    flat = (db * rows, bs)
    order = zs[1:] + zs[:1]

    def remote(src, dst, send, recv, j):
        return pltpu.make_async_remote_copy(
            src_ref=src, dst_ref=dst, send_sem=send, recv_sem=recv,
            device_id=dev(j), device_id_type=pl.DeviceIdType.MESH,
        )

    def copy1(a, zz, yy):
        return remote(
            po.at[a, :, at(zz, yy, 1 - p)], r1.at[a, zz, yy],
            s1.at[a, zz, yy], q1.at[a, zz, yy], sib,
        )

    def local(a, zz, yy):
        return pltpu.make_async_copy(
            po.at[a, :, at(zz, yy, p)], own.at[a, zz, yy], lsem.at[a, zz, yy]
        )

    def copy2(a, zz):
        return remote(t2.at[a, zz], r2.at[a, zz], s2.at[a, zz], q2.at[a, zz], pair)

    def copy3(a, zz, slot):
        return remote(
            t3.at[a, zz], r3.at[a, slot], s3.at[a, zz], q3.at[a, slot], at(zz, y, p)
        )

    def reduce_core(a):
        for yy in (1 - y, y):
            for zz in order:
                copy1(a, zz, yy).start()
                local(a, zz, yy).start()

    def load(ref, *idx):
        return ref.at[idx].reshape(*flat)[...].astype(F32)

    def store(ref, value, *idx):
        ref.at[idx].reshape(*flat)[...] = value.astype(BF16)

    def reduce_pair(a):
        for zz in order:
            copy1(a, zz, 1 - y).wait_recv()
            local(a, zz, 1 - y).wait()
            store(t2, load(own, a, zz, 1 - y) + load(r1, a, zz, 1 - y), a, zz)
            copy2(a, zz).start()

    def reduce_z(a):
        for zz in order:
            copy1(a, zz, y).wait_recv()
            local(a, zz, y).wait()
            copy2(a, zz).wait_recv()
            total = load(own, a, zz, y) + load(r1, a, zz, y) + load(r2, a, zz)
            if zz is zs[0]:
                return total
            store(t3, total, a, zz)
            copy3(a, zz, z).start()

    def reduce_end(a, total, result):
        for zz in zs[1:]:
            copy3(a, zz, zz).wait_recv()
            total += load(r3, a, zz)
        result.reshape(*flat)[...] = total.astype(BF16)
        for zz in order:
            for yy in (0, 1):
                copy1(a, zz, yy).wait_send()
            copy2(a, zz).wait_send()
        for zz in zs[1:]:
            copy3(a, zz, z).wait_send()

    def expand(weights, src, m, dst, dims):
        for s in range(slots):
            minor = lay_ref[m, s] - 3 * third(lay_ref[m, s])
            dst[s] = lax.dot_general(
                src[minor], weights[s], dims, preferred_element_type=F32
            )

    ocopies = [
        pltpu.make_async_copy(src, dst, osem.at[i])
        for i, (src, dst) in enumerate((
            (xg, xg_hbm), (yg, yg_hbm), (hid, hid_hbm), (dup, dup_hbm), (dgt, dgt_hbm)
        ))
    ]
    forward_z(0)
    forward_y(0)
    forward_z(1)
    finish(0)
    ocopies[0].start()
    wcopies[0].wait()
    up = contract(xg, 0, wu, False)
    wcopies[1].wait()
    gate = contract(xg, 1, wg, False)
    sig = 1.0 / (1.0 + jnp.exp(-gate))
    act = gate * sig
    hid.reshape(HB * tt, bs)[...] = (act * up).astype(BF16)
    ocopies[2].start()
    forward_y(1)
    wcopies[2].wait()
    icopy.wait()
    expand(wd, hid, 2, terms, (((1,), (0,)), ((), ())))
    scatter(0, ((2, terms),))
    reduce_core(0)
    finish(1)
    ocopies[1].start()
    d_hidden = contract(yg, 2, wd, True)
    dup.reshape(HB * tt, bs)[...] = (d_hidden * act).astype(BF16)
    dgt.reshape(HB * tt, bs)[...] = (
        d_hidden * up * sig * (1.0 + gate * (1.0 - sig))
    ).astype(BF16)
    ocopies[3].start()
    ocopies[4].start()
    reduce_pair(0)
    expand(wu, dup, 0, terms, NT)
    expand(wg, dgt, 1, terms2, NT)
    scatter(1, ((0, terms), (1, terms2)))
    reduce_core(1)
    total0 = reduce_z(0)
    reduce_pair(1)
    total1 = reduce_z(1)
    reduce_end(0, total0, outp)
    reduce_end(1, total1, dxp)
    for c in pending:
        c.wait_send()
    for c in ocopies:
        c.wait()


def grads_kernel(
    per, lu_ref, lg_ref, ld_ref, cnt_ref, xg, yg, hid, dup, dgt, outp, dxp,
    out, dx, gu, gg, gd,
):
    step = pl.program_id(0)
    db, _, bs = outp.shape

    @pl.when(step == 0)
    def _():
        for c in range(db):
            out[:, c * bs:(c + 1) * bs] = outp[c]
            dx[:, c * bs:(c + 1) * bs] = dxp[c]

    for i in range(per):
        s = step * per + i
        for m, lay, grad in ((0, lu_ref, gu), (1, lg_ref, gg), (2, ld_ref, gd)):
            code = lay[s]
            major = third(code)
            minor = code - 3 * major
            if m == 2:
                lhs, rhs = hid[minor], yg[major]
            else:
                lhs, rhs = xg[major], (dup, dgt)[m][minor]
            lhs = jnp.where(s < cnt_ref[m], lhs, jnp.zeros_like(lhs))
            grad[i] = lax.dot_general(
                lhs, rhs, TN, preferred_element_type=F32
            ).astype(BF16)


def local_part(n, tokens, cotangent, wu, wg, wd, lu, lg, ld, counts):
    rows, width = tokens.shape
    slots, bs, _ = wu.shape
    db, tt, nz = width // bs, n * rows, n // 4
    counts = counts.reshape(3)
    vm = pl.BlockSpec(memory_space=pltpu.VMEM)
    sm = pl.BlockSpec(memory_space=pltpu.SMEM)
    hbm = pl.BlockSpec(memory_space=pltpu.HBM)
    shape = jax.ShapeDtypeStruct
    dma = pltpu.SemaphoreType.DMA
    part = (nz, db, rows, bs)
    xg, yg, hid, dup, dgt, outp, dxp = pl.pallas_call(
        functools.partial(layer_kernel, n),
        out_shape=[shape((db, n, rows, bs), BF16)] * 2
        + [shape((HB, tt, bs), BF16)] * 3
        + [shape((db, rows, bs), BF16)] * 2,
        in_specs=[hbm] * 9,
        out_specs=[hbm] * 5 + [vm] * 2,
        scratch_shapes=[
            pltpu.VMEM((db, n, rows, bs), BF16),
            pltpu.VMEM((db, n, rows, bs), BF16),
            pltpu.VMEM((HB, tt, bs), BF16),
            pltpu.VMEM((HB, tt, bs), BF16),
            pltpu.VMEM((HB, tt, bs), BF16),
            pltpu.SMEM((3, slots), jnp.int32),
            pltpu.SMEM((3,), jnp.int32),
            pltpu.VMEM((rows, width), BF16),
            pltpu.VMEM((rows, width), BF16),
            pltpu.VMEM((slots, bs, bs), BF16),
            pltpu.VMEM((slots, bs, bs), BF16),
            pltpu.VMEM((slots, bs, bs), BF16),
            pltpu.VMEM((slots, HB * tt, bs), BF16),
            pltpu.VMEM((slots + 1, tt, bs), F32),
            pltpu.VMEM((slots + 1, tt, bs), F32),
            pltpu.VMEM((3, 8, 256), jnp.int32),
            pltpu.SMEM((3, 8, 256), jnp.int32),
            pltpu.VMEM((2, db, n, rows, bs), BF16),
            pltpu.VMEM((2, nz, 2, db, rows, bs), BF16),
            pltpu.VMEM((2, nz, 2, db, rows, bs), BF16),
            pltpu.VMEM((2,) + part, BF16),
            pltpu.VMEM((2,) + part, BF16),
            pltpu.VMEM((2,) + part, BF16),
            pltpu.VMEM((2,) + part, BF16),
            dma((5,)), dma((6,)), dma((3,)), dma((1,)), dma((2, n)), dma((2, n)),
            dma((2, nz, 2)), dma((2, nz, 2)), dma((2, nz, 2)),
            dma((2, nz)), dma((2, nz)), dma((2, nz)), dma((2, nz)),
        ],
        compiler_params=pltpu.CompilerParams(
            collective_id=0, has_side_effects=True, vmem_limit_bytes=64 << 20
        ),
        name="layer",
    )(lu, lg, ld, counts, tokens, cotangent, wu, wg, wd)
    xg = xg.reshape(db, tt, bs)
    yg = yg.reshape(db, tt, bs)
    per = slots // 4
    block = pl.BlockSpec((per, bs, bs), lambda i: (i, 0, 0))
    row = pl.BlockSpec((rows, width), lambda i: (0, 0))

    def whole(a):
        return pl.BlockSpec(a.shape, lambda i: (0,) * a.ndim)

    rest = (xg, yg, hid, dup, dgt, outp, dxp)
    return pl.pallas_call(
        functools.partial(grads_kernel, per),
        grid=(4,),
        out_shape=[shape((rows, width), BF16)] * 2 + [shape((slots, bs, bs), BF16)] * 3,
        in_specs=[sm] * 4 + [whole(a) for a in rest],
        out_specs=[row, row, block, block, block],
        compiler_params=pltpu.CompilerParams(vmem_limit_bytes=64 << 20),
        name="grads",
    )(lu, lg, ld, counts, *rest)


def solution(mesh):
    n = mesh.shape["tensor"]
    both = ("groups", "tensor")
    return jax.shard_map(
        functools.partial(local_part, n),
        mesh=mesh,
        in_specs=(
            P(both, None), P(both, None),
            P("tensor", None, None), P("tensor", None, None), P("tensor", None, None),
            P("tensor"), P("tensor"), P("tensor"), P(None, "tensor"),
        ),
        out_specs=(
            P(both, None), P(both, None),
            P(both, None, None), P(both, None, None), P(both, None, None),
        ),
        check_vma=False,
    )
```

```python
import functools

import jax
import jax.numpy as jnp
from jax import lax
from jax.experimental import pallas as pl
from jax.experimental.pallas import tpu as pltpu
from jax.sharding import PartitionSpec as P

HB = 3
BF16 = jnp.bfloat16
F32 = jnp.float32
NT = (((1,), (1,)), ((), ()))
TN = (((0,), (0,)), ((), ()))


def third(code):
    return (code * 171) >> 9


def layer_kernel(
    n, lu_hbm, lg_hbm, ld_hbm, cnt_hbm, tok_hbm, cot_hbm, wu_hbm, wg_hbm, wd_hbm,
    xg_hbm, yg_hbm, hid_hbm, dup_hbm, dgt_hbm, outp, dxp,
    xg, yg, hid, dup, dgt, lay_ref, cnt_ref, tok_ref, cot_ref, wu, wg, wd, mx, terms, terms2, inv_v, inv_s, po, own, r1, t2, r2, t3, r3,
    osem, asem, wsem, isem, gsend, grecv, s1, q1, lsem, s2, q2, s3, q3,
):
    nz = n // 4
    db = xg.shape[0]
    rows = xg.shape[2]
    bs = xg.shape[3]
    tt = n * rows
    slots = wu.shape[0]
    me = lax.axis_index("tensor")
    z, y, p = me // 4, (me // 2) % 2, me % 2
    sib = me + 1 - 2 * p
    pair = me + 2 - 4 * y
    low = jnp.minimum(z, nz - 1 - z)

    def ranked(k):
        half = (k + 1) // 2
        beside = z + half if k % 2 else z - half
        beyond = jnp.where(2 * z < nz, z + (k - low), z - (k - low))
        return jnp.where(k <= 2 * low, beside, beyond)

    zs = [z] + [ranked(k) for k in range(1, nz)]

    def at(zz, yy, pp):
        return zz * 4 + yy * 2 + pp

    def dev(j):
        return {"tensor": j}

    acopies = [
        pltpu.make_async_copy(src, dst, asem.at[i])
        for i, (src, dst) in enumerate((
            (tok_hbm, tok_ref), (cot_hbm, cot_ref), (cnt_hbm, cnt_ref),
            (lu_hbm, lay_ref.at[0]), (lg_hbm, lay_ref.at[1]), (ld_hbm, lay_ref.at[2]),
        ))
    ]
    for c in acopies:
        c.start()
    wcopies = [
        pltpu.make_async_copy(src, dst, wsem.at[i])
        for i, (src, dst) in enumerate(((wu_hbm, wu), (wg_hbm, wg), (wd_hbm, wd)))
    ]
    for c in wcopies:
        c.start()

    barrier = pltpu.get_barrier_semaphore()
    for j in [at(zz, y, p) for zz in zs[1:]] + [pair, sib]:
        pl.semaphore_signal(
            barrier, inc=1, device_id=dev(j), device_id_type=pl.DeviceIdType.MESH
        )

    for c in acopies[:2]:
        c.wait()
    for c in range(db):
        xg[c, me] = tok_ref[:, c * bs:(c + 1) * bs]
        yg[c, me] = cot_ref[:, c * bs:(c + 1) * bs]

    pl.semaphore_wait(barrier, nz - 1 + 2)

    gbuf = (xg, yg)
    nsend = [0, 0]
    pending = []

    def gsendto(a, chunk, j):
        c = pltpu.make_async_remote_copy(
            src_ref=gbuf[a].at[:, chunk],
            dst_ref=gbuf[a].at[:, chunk],
            send_sem=gsend.at[a, nsend[a]],
            recv_sem=grecv.at[a, chunk],
            device_id=dev(j),
            device_id_type=pl.DeviceIdType.MESH,
        )
        nsend[a] += 1
        c.start()
        pending.append(c)

    def gwait(a, chunk):
        pltpu.make_async_remote_copy(
            src_ref=gbuf[a].at[:, chunk],
            dst_ref=gbuf[a].at[:, chunk],
            send_sem=gsend.at[a, 0],
            recv_sem=grecv.at[a, chunk],
            device_id=dev(sib),
            device_id_type=pl.DeviceIdType.MESH,
        ).wait_recv()

    for a in range(2):
        for zz in zs[:0:-1]:
            gsendto(a, me, at(zz, y, p))
        gsendto(a, me, pair)
        gsendto(a, me, sib)

    for c in acopies[2:]:
        c.wait()
    lane = lax.broadcasted_iota(jnp.int32, (8, 256), 1)
    for m in range(3):
        tab = jnp.full((8, 256), slots, jnp.int32)
        for s in range(slots):
            code = jnp.where(s < cnt_ref[m], lay_ref[m, s], -1)
            tab = jnp.where(lane == code, s, tab)
        inv_v[m] = tab
    icopy = pltpu.make_async_copy(inv_v, inv_s, isem.at[0])
    icopy.start()
    terms[slots] = jnp.zeros((tt, bs), F32)
    terms2[slots] = jnp.zeros((tt, bs), F32)

    def forward_z(a):
        for zz in zs[1:]:
            gwait(a, at(zz, y, p))
            gsendto(a, at(zz, y, p), pair)
            gsendto(a, at(zz, y, p), sib)

    def forward_y(a):
        for zz in zs:
            gwait(a, at(zz, 1 - y, p))
            gsendto(a, at(zz, 1 - y, p), sib)

    def finish(a):
        for zz in zs:
            gwait(a, at(zz, y, 1 - p))
            gwait(a, at(zz, 1 - y, 1 - p))

    def contract(src, m, weights, transposed):
        view = src.reshape(db, tt, bs)

        def pick(s, carry):
            code = lay_ref[m, s]
            major = third(code)
            minor = jnp.where(s < cnt_ref[m], code - 3 * major, HB)
            rows_s = view[major]
            for h in range(HB):
                mx[s, h * tt:(h + 1) * tt, :] = jnp.where(
                    minor == h, rows_s, jnp.zeros_like(rows_s)
                )
            return carry

        lax.fori_loop(0, slots, pick, 0, unroll=True)
        acc = jnp.zeros((HB * tt, bs), F32)
        for s in range(slots):
            if transposed:
                acc += lax.dot_general(mx[s], weights[s], NT, preferred_element_type=F32)
            else:
                acc += jnp.dot(mx[s], weights[s], preferred_element_type=F32)
        return acc

    def scatter(a, tables):
        pov = po.at[a].reshape(db, tt, bs)

        def place(c, carry):
            total = jnp.zeros((tt, bs), F32)
            for m, source in tables:
                for h in range(HB):
                    total += source[inv_s[m, 0, c * HB + h]]
            pov[c] = total.astype(BF16)
            return carry

        lax.fori_loop(0, db, place, 0, unroll=4)

    flat = (db * rows, bs)
    order = zs[::-1]

    def remote(src, dst, send, recv, j):
        return pltpu.make_async_remote_copy(
            src_ref=src, dst_ref=dst, send_sem=send, recv_sem=recv,
            device_id=dev(j), device_id_type=pl.DeviceIdType.MESH,
        )

    def copy1(a, zz, yy):
        return remote(
            po.at[a, :, at(zz, yy, 1 - p)], r1.at[a, zz, yy],
            s1.at[a, zz, yy], q1.at[a, zz, yy], sib,
        )

    def local(a, zz, yy):
        return pltpu.make_async_copy(
            po.at[a, :, at(zz, yy, p)], own.at[a, zz, yy], lsem.at[a, zz, yy]
        )

    def copy2(a, zz):
        return remote(t2.at[a, zz], r2.at[a, zz], s2.at[a, zz], q2.at[a, zz], pair)

    def copy3(a, zz, slot):
        return remote(
            t3.at[a, zz], r3.at[a, slot], s3.at[a, zz], q3.at[a, slot], at(zz, y, p)
        )

    def reduce_core(a):
        for yy in (1 - y, y):
            for zz in order:
                copy1(a, zz, yy).start()
                local(a, zz, yy).start()

    def load(ref, *idx):
        return ref.at[idx].reshape(*flat)[...].astype(F32)

    def store(ref, value, *idx):
        ref.at[idx].reshape(*flat)[...] = value.astype(BF16)

    def pair_step(a, zz):
        copy1(a, zz, 1 - y).wait_recv()
        local(a, zz, 1 - y).wait()
        store(t2, load(own, a, zz, 1 - y) + load(r1, a, zz, 1 - y), a, zz)
        copy2(a, zz).start()

    def z_step(a, zz):
        copy1(a, zz, y).wait_recv()
        local(a, zz, y).wait()
        copy2(a, zz).wait_recv()
        total = load(own, a, zz, y) + load(r1, a, zz, y) + load(r2, a, zz)
        if zz is not zs[0]:
            store(t3, total, a, zz)
            copy3(a, zz, z).start()
        return total

    def reduce_end(a, total, result):
        for zz in zs[1:]:
            copy3(a, zz, zz).wait_recv()
            total += load(r3, a, zz)
        result.reshape(*flat)[...] = total.astype(BF16)
        for zz in order:
            for yy in (0, 1):
                copy1(a, zz, yy).wait_send()
            copy2(a, zz).wait_send()
        for zz in zs[1:]:
            copy3(a, zz, z).wait_send()

    def expand(weights, src, m, dst, dims):
        for s in range(slots):
            minor = lay_ref[m, s] - 3 * third(lay_ref[m, s])
            dst[s] = lax.dot_general(
                src[minor], weights[s], dims, preferred_element_type=F32
            )

    ocopies = [
        pltpu.make_async_copy(src, dst, osem.at[i])
        for i, (src, dst) in enumerate((
            (xg, xg_hbm), (yg, yg_hbm), (hid, hid_hbm), (dup, dup_hbm), (dgt, dgt_hbm)
        ))
    ]
    forward_z(0)
    forward_z(1)
    forward_y(0)
    finish(0)
    ocopies[0].start()
    wcopies[0].wait()
    up = contract(xg, 0, wu, False)
    wcopies[1].wait()
    gate = contract(xg, 1, wg, False)
    sig = 1.0 / (1.0 + jnp.exp(-gate))
    act = gate * sig
    hid.reshape(HB * tt, bs)[...] = (act * up).astype(BF16)
    ocopies[2].start()
    forward_y(1)
    wcopies[2].wait()
    icopy.wait()
    expand(wd, hid, 2, terms, (((1,), (0,)), ((), ())))
    scatter(0, ((2, terms),))
    reduce_core(0)
    finish(1)
    ocopies[1].start()
    d_hidden = contract(yg, 2, wd, True)
    dup.reshape(HB * tt, bs)[...] = (d_hidden * act).astype(BF16)
    dgt.reshape(HB * tt, bs)[...] = (
        d_hidden * up * sig * (1.0 + gate * (1.0 - sig))
    ).astype(BF16)
    ocopies[3].start()
    ocopies[4].start()
    for zz in order:
        pair_step(0, zz)
    expand(wu, dup, 0, terms, NT)
    expand(wg, dgt, 1, terms2, NT)
    scatter(1, ((0, terms), (1, terms2)))
    reduce_core(1)
    for zz in order:
        total0 = z_step(0, zz)
        pair_step(1, zz)
    for zz in order:
        total1 = z_step(1, zz)
    reduce_end(0, total0, outp)
    reduce_end(1, total1, dxp)
    for c in pending:
        c.wait_send()
    for c in ocopies:
        c.wait()


def grads_kernel(
    per, lu_ref, lg_ref, ld_ref, cnt_ref, xg, yg, hid, dup, dgt, outp, dxp,
    out, dx, gu, gg, gd,
):
    step = pl.program_id(0)
    db, _, bs = outp.shape

    @pl.when(step == 0)
    def _():
        for c in range(db):
            out[:, c * bs:(c + 1) * bs] = outp[c]
            dx[:, c * bs:(c + 1) * bs] = dxp[c]

    for i in range(per):
        s = step * per + i
        for m, lay, grad in ((0, lu_ref, gu), (1, lg_ref, gg), (2, ld_ref, gd)):
            code = lay[s]
            major = third(code)
            minor = code - 3 * major
            if m == 2:
                lhs, rhs = hid[minor], yg[major]
            else:
                lhs, rhs = xg[major], (dup, dgt)[m][minor]
            lhs = jnp.where(s < cnt_ref[m], lhs, jnp.zeros_like(lhs))
            grad[i] = lax.dot_general(
                lhs, rhs, TN, preferred_element_type=F32
            ).astype(BF16)


def local_part(n, tokens, cotangent, wu, wg, wd, lu, lg, ld, counts):
    rows, width = tokens.shape
    slots, bs, _ = wu.shape
    db, tt, nz = width // bs, n * rows, n // 4
    counts = counts.reshape(3)
    vm = pl.BlockSpec(memory_space=pltpu.VMEM)
    sm = pl.BlockSpec(memory_space=pltpu.SMEM)
    hbm = pl.BlockSpec(memory_space=pltpu.HBM)
    shape = jax.ShapeDtypeStruct
    dma = pltpu.SemaphoreType.DMA
    part = (nz, db, rows, bs)
    xg, yg, hid, dup, dgt, outp, dxp = pl.pallas_call(
        functools.partial(layer_kernel, n),
        out_shape=[shape((db, n, rows, bs), BF16)] * 2
        + [shape((HB, tt, bs), BF16)] * 3
        + [shape((db, rows, bs), BF16)] * 2,
        in_specs=[hbm] * 9,
        out_specs=[hbm] * 5 + [vm] * 2,
        scratch_shapes=[
            pltpu.VMEM((db, n, rows, bs), BF16),
            pltpu.VMEM((db, n, rows, bs), BF16),
            pltpu.VMEM((HB, tt, bs), BF16),
            pltpu.VMEM((HB, tt, bs), BF16),
            pltpu.VMEM((HB, tt, bs), BF16),
            pltpu.SMEM((3, slots), jnp.int32),
            pltpu.SMEM((3,), jnp.int32),
            pltpu.VMEM((rows, width), BF16),
            pltpu.VMEM((rows, width), BF16),
            pltpu.VMEM((slots, bs, bs), BF16),
            pltpu.VMEM((slots, bs, bs), BF16),
            pltpu.VMEM((slots, bs, bs), BF16),
            pltpu.VMEM((slots, HB * tt, bs), BF16),
            pltpu.VMEM((slots + 1, tt, bs), F32),
            pltpu.VMEM((slots + 1, tt, bs), F32),
            pltpu.VMEM((3, 8, 256), jnp.int32),
            pltpu.SMEM((3, 8, 256), jnp.int32),
            pltpu.VMEM((2, db, n, rows, bs), BF16),
            pltpu.VMEM((2, nz, 2, db, rows, bs), BF16),
            pltpu.VMEM((2, nz, 2, db, rows, bs), BF16),
            pltpu.VMEM((2,) + part, BF16),
            pltpu.VMEM((2,) + part, BF16),
            pltpu.VMEM((2,) + part, BF16),
            pltpu.VMEM((2,) + part, BF16),
            dma((5,)), dma((6,)), dma((3,)), dma((1,)), dma((2, n)), dma((2, n)),
            dma((2, nz, 2)), dma((2, nz, 2)), dma((2, nz, 2)),
            dma((2, nz)), dma((2, nz)), dma((2, nz)), dma((2, nz)),
        ],
        compiler_params=pltpu.CompilerParams(
            collective_id=0, has_side_effects=True, vmem_limit_bytes=64 << 20
        ),
        name="layer",
    )(lu, lg, ld, counts, tokens, cotangent, wu, wg, wd)
    xg = xg.reshape(db, tt, bs)
    yg = yg.reshape(db, tt, bs)
    per = slots // 4
    block = pl.BlockSpec((per, bs, bs), lambda i: (i, 0, 0))
    row = pl.BlockSpec((rows, width), lambda i: (0, 0))

    def whole(a):
        return pl.BlockSpec(a.shape, lambda i: (0,) * a.ndim)

    rest = (xg, yg, hid, dup, dgt, outp, dxp)
    return pl.pallas_call(
        functools.partial(grads_kernel, per),
        grid=(4,),
        out_shape=[shape((rows, width), BF16)] * 2 + [shape((slots, bs, bs), BF16)] * 3,
        in_specs=[sm] * 4 + [whole(a) for a in rest],
        out_specs=[row, row, block, block, block],
        compiler_params=pltpu.CompilerParams(vmem_limit_bytes=64 << 20),
        name="grads",
    )(lu, lg, ld, counts, *rest)


def solution(mesh):
    n = mesh.shape["tensor"]
    both = ("groups", "tensor")
    return jax.shard_map(
        functools.partial(local_part, n),
        mesh=mesh,
        in_specs=(
            P(both, None), P(both, None),
            P("tensor", None, None), P("tensor", None, None), P("tensor", None, None),
            P("tensor"), P("tensor"), P("tensor"), P(None, "tensor"),
        ),
        out_specs=(
            P(both, None), P(both, None),
            P(both, None, None), P(both, None, None), P(both, None, None),
        ),
        check_vma=False,
    )
```
